512 devices in a mesh: ctx: 64 (over y, z_lo, core), dp: 8 (over z_hi, x).
Axes of the slice: x: 4, y: 4, z: 16 (z_hi: 2, z_lo: 8; z = z_hi * 8 + z_lo), core: 2. Of those that a mesh axis runs over, the one named last changes fastest.
Arguments:
- tokens: bfloat16 [8, 8192, 4096], P('dp', 'ctx'), may hold values from -64 to 64
- stretch_table: int32 [64, 2], replicated, may hold values from 0 to 127, as said below
- query_weight: bfloat16 [4096, 512], P(('ctx', 'dp')), may hold values from -1 to 1
- key_weight: bfloat16 [4096, 128], P(('ctx', 'dp')), may hold values from -1 to 1
- value_weight: bfloat16 [4096, 128], P(('ctx', 'dp')), may hold values from -0.09375 to 0.09375
Outputs:
- attended: bfloat16 [8, 8192, 512], P('dp', 'ctx')
The draws below stay inside these ranges and needn't reach their ends.
Inputs may be any that keep to these rules, and one draw needn't show every extreme that they name: `stretch_table`: row r names stretches c and 127 - c for some c < 64, in either order; every stretch of the sequence is named once.
All inputs are finite; a program needn't handle non-finite values.
Results may differ from the reference program's by a relative error of at most 0.012.
Values may be sent and summed in bfloat16 or wider, within the bound.
No kernel may reach another device: no remote copies, remote signals or barrier semaphores. Data moves between devices by JAX's collectives and lax.ppermute only.
A program may use at most 64 MiB of HBM per device.

```python
import math
import jax
import jax.numpy as jnp
from jax import lax

D = 4096
HQ = 4
HEAD = 128
TOK_DEV = 128
STRETCH = 64
SEQ = 8192
STRETCHES = 128
GROUPS = 8


def clipped(key, shape):
    return jnp.clip(jax.random.normal(key, shape, jnp.float32), -6.0, 6.0)


def draw_tokens(key, part):
    base = clipped(jax.random.fold_in(key, 1), (GROUPS, SEQ, D))
    return base.astype(jnp.bfloat16)


def draw_query_weight(key, part):
    own_noise = clipped(jax.random.fold_in(key, 11), (D, HQ * HEAD))
    return (1.9 * own_noise / math.sqrt(D)).astype(jnp.bfloat16)


def draw_key_weight(key, part):
    own_noise = clipped(jax.random.fold_in(key, 12), (D, HEAD))
    return (1.9 * own_noise / math.sqrt(D)).astype(jnp.bfloat16)


def draw_stretch_table(key, part):
    cycle_size = STRETCHES // 2
    order = jax.random.permutation(jax.random.fold_in(key, 21), cycle_size).astype(jnp.int32)
    flips = jax.random.randint(jax.random.fold_in(key, 22), (cycle_size,), 0, 2, jnp.int32)
    mirror = (STRETCHES - 1 - order).astype(jnp.int32)
    first_slot = jnp.where(flips == 1, mirror, order)
    second_slot = jnp.where(flips == 1, order, mirror)
    return jnp.stack([first_slot, second_slot], axis=1).astype(jnp.int32)


def block_levels(own_key, dims, split, least, largest):
    gain = 1.0
    for axis_at, shards_of in split:
        draws = jax.random.uniform(jax.random.fold_in(jax.random.fold_in(own_key, 6), axis_at), (shards_of,), jnp.float32, least / len(split), largest / len(split))
        gain = gain * jnp.repeat(jnp.exp(draws), dims[axis_at] // shards_of).reshape((-1,) + (1,) * (len(dims) - 1 - axis_at))
    return gain


def normal_values(stream_key, extent, scale, limit, split=(), held_as=jnp.bfloat16):
    values = jax.random.normal(stream_key, extent, jnp.float32) * scale
    if len(split) > 0:
        values = block_levels(stream_key, extent, split, -0.22, 0.18) * values
    return jnp.clip(values, min=-limit, max=limit).astype(held_as)


def setup_inputs(seed: int = 0) -> dict:
    streams_of = jax.random.split(jax.random.key(seed), 6)
    tokens = draw_tokens(jax.random.fold_in(streams_of[5], 71), 0)
    stretch_table = draw_stretch_table(jax.random.fold_in(streams_of[5], 71), 0)
    query_weight = draw_query_weight(jax.random.fold_in(streams_of[5], 71), 0)
    key_weight = draw_key_weight(jax.random.fold_in(streams_of[5], 71), 0)
    value_weight = normal_values(streams_of[4], (D, HEAD), D ** -0.5, 0.09375, ((0, 512),))
    return {"tokens": tokens, "stretch_table": stretch_table, "query_weight": query_weight, "key_weight": key_weight, "value_weight": value_weight}


rope_base = 500000.0
masked_fill = -1e+30

def rotate(vectors, positions):
    head_width = vectors.shape[-1]
    half_width = head_width // 2
    frequency = rope_base ** (-(jnp.arange(half_width, dtype=jnp.float32) * 2.0 / head_width))
    angles = positions.astype(jnp.float32)[:, None] * frequency[None, :]
    cosine = jnp.cos(angles)[:, None, :]
    sine_part = jnp.sin(angles)[:, None, :]
    first_half = vectors[..., :half_width]
    second_half = vectors[..., half_width:]
    return jnp.concatenate([first_half * cosine - second_half * sine_part, second_half * cosine + first_half * sine_part], axis=-1)

def reference(tokens, stretch_table, query_weight, key_weight, value_weight):
    row_index = jnp.arange(SEQ, dtype=jnp.int32)
    device = row_index // TOK_DEV
    slot_index = row_index % TOK_DEV // STRETCH
    positions = (stretch_table[device, slot_index] * STRETCH + row_index % STRETCH).astype(jnp.int32)
    blocks = SEQ // STRETCH
    score_scale = 1.0 / math.sqrt(HEAD)

    def one_group(token_rows):
        query_full = jnp.dot(token_rows, query_weight, preferred_element_type=jnp.float32)
        key_full = jnp.dot(token_rows, key_weight, preferred_element_type=jnp.float32)
        value_full = jnp.dot(token_rows, value_weight, preferred_element_type=jnp.float32)
        queries = rotate(query_full.reshape(SEQ, HQ, HEAD), positions).astype(jnp.bfloat16)
        keys_all = rotate(key_full[:, None, :], positions)[:, 0, :].astype(jnp.bfloat16)
        values_all = value_full.astype(jnp.bfloat16)
        keys_wide = keys_all.astype(jnp.float32)
        values_wide = values_all.astype(jnp.float32)
        query_blocks = queries.reshape(blocks, STRETCH, HQ, HEAD)
        position_blocks = positions.reshape(blocks, STRETCH)

        def attend(pair):
            query_block, query_pos = pair
            scores = jnp.einsum('qhd,kd->hqk', query_block.astype(jnp.float32), keys_wide) * score_scale
            allowed = positions[None, None, :] <= query_pos[None, :, None]
            scores = jnp.where(allowed, scores, masked_fill)
            row_top = lax.optimization_barrier(jnp.max(scores, axis=-1, keepdims=True))
            rounded = jnp.where(allowed, jnp.exp(scores - row_top), 0.0).astype(jnp.bfloat16)
            rounded = lax.optimization_barrier(rounded)
            probabilities = rounded.astype(jnp.float32)
            totals = lax.optimization_barrier(jnp.sum(probabilities, axis=-1))
            mixed = jnp.einsum('hqk,kd->qhd', probabilities, values_wide) / jnp.transpose(totals)[:, :, None]
            return mixed.reshape(STRETCH, HQ * HEAD).astype(jnp.bfloat16)
        return lax.map(attend, (query_blocks, position_blocks)).reshape(SEQ, HQ * HEAD)
    return lax.map(one_group, tokens)
```

```python
import math

import jax
import jax.numpy as jnp
from jax import lax
from jax.experimental import pallas as pl
from jax.experimental.pallas import tpu as pltpu
from jax.sharding import Mesh, PartitionSpec as P

rope_base = 500000.0
masked_fill = -1e30
HEAD = 128
HEADS = 4
STRETCH = 64
ROWS = 128
KEYS = 2048
CHUNK = 512
score_scale = 1.0 / math.sqrt(HEAD)
exponent_scale = score_scale * math.log2(math.e)

vmem = pl.BlockSpec(memory_space=pltpu.VMEM)
smem = pl.BlockSpec(memory_space=pltpu.SMEM)


def swap(value, axis, size, distance):
    return lax.ppermute(value, axis, [(i, i ^ distance) for i in range(size)])


def spread(value, axis, size):
    copies = jnp.broadcast_to(value[None], (size,) + value.shape)
    return lax.all_to_all(copies, axis, 0, 0)


def angle_tables(positions):
    half = HEAD // 2
    frequency = rope_base ** (-(jnp.arange(half, dtype=jnp.float32) * 2.0 / HEAD))
    angles = positions.astype(jnp.float32)[:, None] * frequency[None, :]
    cosine = jnp.cos(angles)
    sine = jnp.sin(angles)
    return (
        jnp.concatenate([cosine, cosine], axis=1),
        jnp.concatenate([-sine, sine], axis=1),
    )


def key_value_kernel(parts, cosine, sine, out):
    total = parts[0] + parts[1] + parts[2] + parts[3]
    key = total[:, :HEAD]
    turned = key * cosine[...] + pltpu.roll(key, HEAD // 2, 1) * sine[...]
    out[:, :HEAD] = turned.astype(jnp.bfloat16)
    out[:, HEAD:] = total[:, HEAD:].astype(jnp.bfloat16)


def query_kernel(parts, cosine, sine, out):
    for head in range(HEADS):
        span = slice(head * HEAD, (head + 1) * HEAD)
        total = parts[0, :, span] + parts[1, :, span] + parts[2, :, span] + parts[3, :, span]
        turned = total * cosine[...] + pltpu.roll(total, HEAD // 2, 1) * sine[...]
        turned = turned.astype(jnp.bfloat16)
        for slot in range(2):
            row = (slot * HEADS + head) * STRETCH
            out[row : row + STRETCH, :] = turned[slot * STRETCH : (slot + 1) * STRETCH]


def attention_kernel(plan, query, own_near, own_far, other_near, other_far, out, keys, values, scores):
    pieces = (own_near, own_far, other_near, other_far)
    values[:, HEAD:] = jnp.ones((KEYS, HEAD), jnp.bfloat16)
    for index in range(KEYS // STRETCH):
        piece = pieces[index // 8]
        source = (index % 8) * STRETCH
        target = pl.multiple_of(plan[index] * STRETCH, STRETCH)
        keys[pl.ds(target, STRETCH), :] = piece[source : source + STRETCH, :HEAD]
        values[pl.ds(target, STRETCH), :HEAD] = piece[source : source + STRETCH, HEAD:]
    rows = HEADS * STRETCH
    stretch_row = lax.broadcasted_iota(jnp.int32, (rows, CHUNK), 0) % STRETCH
    lane = lax.broadcasted_iota(jnp.int32, (rows, CHUNK), 1)
    small_lane = lax.broadcasted_iota(jnp.int32, (STRETCH, HEAD), 1)
    own_row = plan[40]
    for index in range(8):
        peer = index // 2
        slot = index % 2
        full = plan[32 + index] * STRETCH
        here = (own_row == peer).astype(jnp.int32)
        chunks = (full + here * STRETCH + CHUNK - 1) // CHUNK
        limit = lane - stretch_row * here
        q = query[index * rows : (index + 1) * rows, :]

        def score(chunk, running, q=q, limit=limit, full=full, here=here):
            start = pl.multiple_of(chunk * CHUNK, CHUNK)
            s = lax.dot_general(
                q, keys[pl.ds(start, CHUNK), :], (((1,), (1,)), ((), ())),
                preferred_element_type=jnp.float32,
            )
            s = jnp.where(limit < full + here - start, s, masked_fill)
            scores[chunk] = s
            for part in range(CHUNK // HEAD):
                running = jnp.maximum(running, s[:, part * HEAD : (part + 1) * HEAD])
            return running

        running = lax.fori_loop(
            0, chunks, score, jnp.full((rows, HEAD), masked_fill, jnp.float32)
        )
        top = jnp.max(running, axis=1, keepdims=True)

        def mix(chunk, acc, top=top):
            start = pl.multiple_of(chunk * CHUNK, CHUNK)
            p = jnp.exp2((scores[chunk] - top) * exponent_scale).astype(jnp.bfloat16)
            return acc + jnp.dot(
                p, values[pl.ds(start, CHUNK), :], preferred_element_type=jnp.float32
            )

        acc = lax.fori_loop(0, chunks, mix, jnp.zeros((rows, 2 * HEAD), jnp.float32))
        total = acc[:, HEAD:]
        mixed = acc[:, :HEAD] / jnp.where(total > 0.0, total, 1.0)
        stats = jnp.zeros((STRETCH, HEAD), jnp.float32)
        where_row = slice(slot * STRETCH, (slot + 1) * STRETCH)
        for head in range(HEADS):
            span = slice(head * STRETCH, (head + 1) * STRETCH)
            out[peer, where_row, head * HEAD : (head + 1) * HEAD] = mixed[span].astype(
                jnp.bfloat16
            )
            for kind, whole in enumerate((jnp.broadcast_to(top[span], (STRETCH, HEAD)), total[span])):
                rest = whole
                for digit in range(3):
                    part = rest.astype(jnp.bfloat16).astype(jnp.float32)
                    stats = jnp.where(small_lane == head * 6 + kind * 3 + digit, part, stats)
                    rest = rest - part
        out[peer, where_row, HEADS * HEAD :] = stats.astype(jnp.bfloat16)


def combine_kernel(parts, out):
    stats = [parts[peer, :, HEADS * HEAD :].astype(jnp.float32) for peer in range(4)]
    for head in range(HEADS):
        tops = []
        totals = []
        for peer in range(4):
            column = [stats[peer][:, head * 6 + k : head * 6 + k + 1] for k in range(6)]
            tops.append(column[0] + column[1] + column[2])
            totals.append(column[3] + column[4] + column[5])
        top = jnp.maximum(jnp.maximum(tops[0], tops[1]), jnp.maximum(tops[2], tops[3]))
        weights = [jnp.exp2((tops[k] - top) * exponent_scale) * totals[k] for k in range(4)]
        whole = weights[0] + weights[1] + weights[2] + weights[3]
        mixed = 0.0
        for peer in range(4):
            share = jnp.broadcast_to(weights[peer] / whole, (ROWS, HEAD))
            mixed += share * parts[peer, :, head * HEAD : (head + 1) * HEAD].astype(jnp.float32)
        out[:, head * HEAD : (head + 1) * HEAD] = mixed.astype(jnp.bfloat16)


def on_device(tokens, stretch_table, query_weight, key_weight, value_weight):
    bf16, f32 = jnp.bfloat16, jnp.float32
    y = lax.axis_index("y")
    zl = lax.axis_index("zl")
    core = lax.axis_index("core")
    rows = tokens[0]
    sliced = lax.all_to_all(
        jnp.transpose(rows.reshape(ROWS, 4, 1024), (1, 0, 2)), "y", 0, 0
    ).reshape(4 * ROWS, 1024)
    own = jnp.concatenate([key_weight, value_weight, query_weight], axis=1)
    along_z = spread(own, ("zl", "zh"), 16)
    along_x = spread(along_z, "x", 4)
    across = swap(along_x, "core", 2, 1)
    both = jnp.where(core == 0, jnp.stack([along_x, across]), jnp.stack([across, along_x]))
    weight = jnp.transpose(both.reshape(2, 4, 8, 2, 8, 768), (2, 0, 3, 1, 4, 5)).reshape(1024, 768)

    table = stretch_table.reshape(4, 8, 2, 2)
    own_stretches = table[y, zl, core]
    offsets = jnp.arange(STRETCH, dtype=jnp.int32)
    positions = (own_stretches[:, None] * STRETCH + offsets[None, :]).reshape(ROWS)
    cosine, sine = angle_tables(positions)
    r = jnp.arange(16, dtype=jnp.int32)
    key_zl = zl ^ (4 * (r & 1)) ^ (2 * ((r >> 1) & 1)) ^ ((r >> 2) & 1)
    key_core = core ^ (r >> 3)
    key_index = y * 16 + key_zl * 2 + key_core
    device = jnp.arange(64, dtype=jnp.int32)
    pick = key_index[:, None, None] == device[None, :, None]
    key_stretch = jnp.sum(jnp.where(pick, stretch_table[None], 0), axis=1).reshape(32)
    query_index = jnp.arange(4, dtype=jnp.int32) * 16 + zl * 2 + core
    pick = query_index[:, None, None] == device[None, :, None]
    query_stretch = jnp.sum(jnp.where(pick, stretch_table[None], 0), axis=1).reshape(8)
    ranks = jnp.sum((key_stretch[None, :] < key_stretch[:, None]).astype(jnp.int32), axis=1)
    counts = jnp.sum((key_stretch[None, :] < query_stretch[:, None]).astype(jnp.int32), axis=1)
    plan = jnp.concatenate([ranks, counts, jnp.full((8,), y, jnp.int32)])

    part = jnp.dot(sliced, weight[:, : 2 * HEAD], preferred_element_type=f32)
    part = lax.all_to_all(part.reshape(4, ROWS, 2 * HEAD), "y", 0, 0)
    key_value = pl.pallas_call(
        key_value_kernel,
        out_shape=jax.ShapeDtypeStruct((ROWS, 2 * HEAD), bf16),
        in_specs=[vmem] * 3,
        out_specs=vmem,
        name="key_value",
    )(part, cosine, sine)

    step = swap(key_value, "zl", 8, 4)
    step = jnp.concatenate([key_value, step], axis=0)
    near = jnp.concatenate([step, swap(step, "zl", 8, 2)], axis=0)
    far = swap(near, "zl", 8, 1)
    other_near = swap(near, "core", 2, 1)
    other_far = swap(far, "core", 2, 1)

    part = jnp.dot(sliced, weight[:, 2 * HEAD :], preferred_element_type=f32)
    part = lax.all_to_all(part.reshape(4, ROWS, HEADS * HEAD), "y", 0, 0)
    query = pl.pallas_call(
        query_kernel,
        out_shape=jax.ShapeDtypeStruct((HEADS * ROWS, HEAD), bf16),
        in_specs=[vmem] * 3,
        out_specs=vmem,
        name="query",
    )(part, cosine, sine)
    query = spread(query, "y", 4).reshape(4 * HEADS * ROWS, HEAD)

    partial = pl.pallas_call(
        attention_kernel,
        out_shape=jax.ShapeDtypeStruct((4, ROWS, HEADS * HEAD + HEAD), bf16),
        in_specs=[smem] + [vmem] * 5,
        out_specs=vmem,
        scratch_shapes=[
            pltpu.VMEM((KEYS, HEAD), bf16),
            pltpu.VMEM((KEYS, 2 * HEAD), bf16),
            pltpu.VMEM((KEYS // CHUNK, HEADS * STRETCH, CHUNK), f32),
        ],
        name="attention",
    )(plan, query, near, far, other_near, other_far)
    partial = lax.all_to_all(partial, "y", 0, 0)
    attended = pl.pallas_call(
        combine_kernel,
        out_shape=jax.ShapeDtypeStruct((ROWS, HEADS * HEAD), bf16),
        in_specs=[vmem],
        out_specs=vmem,
        name="combine",
    )(partial)
    return attended[None]


def solution(mesh):
    fine = Mesh(mesh.devices.reshape(4, 8, 2, 2, 4), ("y", "zl", "core", "zh", "x"))
    ctx = ("y", "zl", "core")
    dp = ("zh", "x")
    placed = (
        P(dp, ctx, None),
        P(),
        P(ctx + dp, None),
        P(ctx + dp, None),
        P(ctx + dp, None),
    )
    return jax.shard_map(
        on_device, mesh=fine, in_specs=placed, out_specs=P(dp, ctx, None), check_vma=False
    )
```

```python
import math

import jax
import jax.numpy as jnp
from jax import lax
from jax.experimental import pallas as pl
from jax.experimental.pallas import tpu as pltpu
from jax.sharding import Mesh, PartitionSpec as P

rope_base = 500000.0
masked_fill = -1e30
HEAD = 128
HEADS = 4
STRETCH = 64
ROWS = 128
KEYS = 2048
CHUNK = 512
score_scale = 1.0 / math.sqrt(HEAD)
exponent_scale = score_scale * math.log2(math.e)

vmem = pl.BlockSpec(memory_space=pltpu.VMEM)
smem = pl.BlockSpec(memory_space=pltpu.SMEM)


def swap(value, axis, size, distance):
    return lax.ppermute(value, axis, [(i, i ^ distance) for i in range(size)])


def spread(value, axis, size):
    copies = jnp.broadcast_to(value[None], (size,) + value.shape)
    return lax.all_to_all(copies, axis, 0, 0)


def angle_tables(positions):
    half = HEAD // 2
    frequency = rope_base ** (-(jnp.arange(half, dtype=jnp.float32) * 2.0 / HEAD))
    angles = positions.astype(jnp.float32)[:, None] * frequency[None, :]
    cosine = jnp.cos(angles)
    sine = jnp.sin(angles)
    return (
        jnp.concatenate([cosine, cosine], axis=1),
        jnp.concatenate([-sine, sine], axis=1),
    )


def key_value_kernel(parts, cosine, sine, out):
    total = parts[0] + parts[1] + parts[2] + parts[3]
    key = total[:, :HEAD]
    turned = key * cosine[...] + pltpu.roll(key, HEAD // 2, 1) * sine[...]
    out[:, :HEAD] = turned.astype(jnp.bfloat16)
    out[:, HEAD:] = total[:, HEAD:].astype(jnp.bfloat16)


def query_kernel(flip, parts, cosine, sine, out):
    for head in range(HEADS):
        span = slice(head * HEAD, (head + 1) * HEAD)
        total = parts[0, :, span] + parts[1, :, span] + parts[2, :, span] + parts[3, :, span]
        turned = total * cosine[...] + pltpu.roll(total, HEAD // 2, 1) * sine[...]
        turned = turned.astype(jnp.bfloat16)
        for slot in range(2):
            level = slot ^ flip[0]
            row = pl.multiple_of((level * HEADS + head) * STRETCH, STRETCH)
            piece = turned[slot * STRETCH : (slot + 1) * STRETCH]
            for copy in range(4):
                out[copy, pl.ds(row, STRETCH), :] = piece


def project_kernel(where, rows0, rows1, rows2, rows3, mine, across, out, weight):
    y = where[0]
    core = where[1]
    width = out.shape[2]
    first = 0 if width == 2 * HEAD else 2 * HEAD
    for far, source in enumerate((mine, across)):
        base = (core ^ far) * 64
        for group in range(8):
            for half in range(2):
                rows = [
                    source[x, (group * 2 + half) * 8 : (group * 2 + half) * 8 + 8, first : first + width]
                    for x in range(4)
                ]
                target = pl.multiple_of(group * 128 + half * 32 + base, 32)
                weight[pl.ds(target, 32), :] = jnp.concatenate(rows, axis=0)
    for shift, rows in enumerate((rows0, rows1, rows2, rows3)):
        out[(y + 4 - shift) % 4] = jnp.dot(
            rows[...], weight[...], preferred_element_type=jnp.float32
        )


def order_kernel(plan, own_near, own_far, other_near, other_far, keys, values):
    pieces = (own_near, own_far, other_near, other_far)
    values[:, HEAD:] = jnp.ones((KEYS, HEAD), jnp.bfloat16)
    for index in range(KEYS // STRETCH):
        piece = pieces[index // 8]
        source = (index % 8) * STRETCH
        target = pl.multiple_of(plan[index] * STRETCH, STRETCH)
        keys[pl.ds(target, STRETCH), :] = piece[source : source + STRETCH, :HEAD]
        values[pl.ds(target, STRETCH), :HEAD] = piece[source : source + STRETCH, HEAD:]


def scores_of(q, keys, low_key):
    return lax.dot_general(
        q, keys[low_key : low_key + CHUNK, :], (((1,), (1,)), ((), ())),
        preferred_element_type=jnp.float32,
    )


def attend_peer(plan, peer, q_low, q_high, keys, values, scores, write):
    rows = HEADS * STRETCH
    here = (plan[40] == peer).astype(jnp.int32)
    in_stretch = lax.broadcasted_iota(jnp.int32, (rows, HEAD), 0) % STRETCH + 1
    lane = lax.broadcasted_iota(jnp.int32, (rows, HEAD), 1)
    slack = in_stretch * here - lane
    small_lane = lax.broadcasted_iota(jnp.int32, (STRETCH, HEAD), 1)
    tops = []
    for level, q in enumerate((q_low, q_high)):
        full = (plan[32 + 2 * peer + level] - 16 * level) * STRETCH
        running = jnp.full((rows, HEAD), -1e20, jnp.float32)
        for block in range(2 * (1 + level)):
            masked = level == 0 or block >= 2
            s = scores_of(q, keys, block * CHUNK)
            for part in range(CHUNK // HEAD):
                lanes = slice(part * HEAD, (part + 1) * HEAD)
                t = s[:, lanes]
                if masked:
                    start = (block % 2) * CHUNK + part * HEAD
                    t = jnp.where(slack > start - full, t, masked_fill)
                scores[2 * level + block, :, lanes] = t
                running = jnp.maximum(running, t)
        tops.append(jnp.max(running, axis=1, keepdims=True))
    for level in range(2):
        top = tops[level]
        acc = jnp.zeros((rows, 2 * HEAD), jnp.float32)
        for block in range(2 * (1 + level)):
            p = jnp.exp2((scores[2 * level + block] - top) * exponent_scale).astype(jnp.bfloat16)
            acc = acc + jnp.dot(
                p, values[block * CHUNK : (block + 1) * CHUNK, :], preferred_element_type=jnp.float32
            )
        total = acc[:, HEAD:]
        mixed = acc[:, :HEAD] / jnp.where(total > 0.0, total, 1.0)
        stats = jnp.zeros((STRETCH, HEAD), jnp.float32)
        row = pl.multiple_of((level ^ plan[41 + peer]) * STRETCH, STRETCH)
        for head in range(HEADS):
            span = slice(head * STRETCH, (head + 1) * STRETCH)
            write(row, slice(head * HEAD, (head + 1) * HEAD), mixed[span].astype(jnp.bfloat16))
            for kind, whole in enumerate((jnp.broadcast_to(top[span], (STRETCH, HEAD)), total[span])):
                rest = whole
                for digit in range(3):
                    part = rest.astype(jnp.bfloat16).astype(jnp.float32)
                    stats = jnp.where(small_lane == head * 6 + kind * 3 + digit, part, stats)
                    rest = rest - part
        write(row, slice(HEADS * HEAD, HEADS * HEAD + HEAD), stats.astype(jnp.bfloat16))


def peers_kernel(plan, query, keys, values, out, scores):
    rows = HEADS * STRETCH
    own = plan[40]
    out[own] = jnp.zeros(out.shape[1:], jnp.bfloat16)

    def body(shift, carried):
        peer = (own + shift) % 4

        def write(row, lanes, value):
            out[peer, pl.ds(row, STRETCH), lanes] = value

        attend_peer(
            plan, peer, query[peer, :rows, :], query[peer, rows:, :], keys, values, scores, write
        )
        return carried

    lax.fori_loop(1, 4, body, 0)


def own_kernel(plan, query, keys, values, out, scores):
    rows = HEADS * STRETCH

    def write(row, lanes, value):
        out[pl.ds(row, STRETCH), lanes] = value

    attend_peer(
        plan, plan[40], query[0, :rows, :], query[0, rows:, :], keys, values, scores, write
    )


def combine_kernel(plan, parts, own, out):
    y = plan[40]
    lane = lax.broadcasted_iota(jnp.int32, (HEAD, 8 * HEAD), 0)
    group = lax.broadcasted_iota(jnp.int32, (HEAD, 8 * HEAD), 1) // HEAD
    pick = (lane // 3 == group).astype(jnp.float32).astype(jnp.bfloat16)
    results = [jnp.where(y == peer, own[...], parts[peer]) for peer in range(4)]
    spread_stats = [
        jnp.dot(result[:, HEADS * HEAD :], pick, preferred_element_type=jnp.float32)
        for result in results
    ]
    for head in range(HEADS):
        tops = [w[:, 2 * head * HEAD : (2 * head + 1) * HEAD] for w in spread_stats]
        totals = [w[:, (2 * head + 1) * HEAD : (2 * head + 2) * HEAD] for w in spread_stats]
        top = jnp.maximum(jnp.maximum(tops[0], tops[1]), jnp.maximum(tops[2], tops[3]))
        weights = [jnp.exp2((tops[k] - top) * exponent_scale) * totals[k] for k in range(4)]
        whole = weights[0] + weights[1] + weights[2] + weights[3]
        mixed = 0.0
        for peer in range(4):
            mixed += weights[peer] * results[peer][:, head * HEAD : (head + 1) * HEAD].astype(jnp.float32)
        out[:, head * HEAD : (head + 1) * HEAD] = (mixed / whole).astype(jnp.bfloat16)


def after(value, *others):
    return lax.optimization_barrier((value,) + others)[0]


def on_device(tokens, stretch_table, query_weight, key_weight, value_weight):
    bf16, f32 = jnp.bfloat16, jnp.float32
    y = lax.axis_index("y")
    zl = lax.axis_index("zl")
    core = lax.axis_index("core")
    rows = tokens[0]
    own = jnp.concatenate([key_weight, value_weight, query_weight], axis=1)
    along_z = spread(own, ("zl", "zh"), 16)
    sliced = []
    for shift in range(4):
        target = (y + shift) % 4
        piece = lax.dynamic_slice_in_dim(rows, target * 1024, 1024, 1)
        if shift:
            piece = lax.ppermute(piece, "y", [(i, (i + shift) % 4) for i in range(4)])
        sliced.append(piece)
    along_z = after(along_z, *sliced)
    along_x = spread(along_z, "x", 4).reshape(4, ROWS, 768)
    across = swap(along_x, "core", 2, 1)

    table = stretch_table.reshape(4, 8, 2, 2)
    own_stretches = table[y, zl, core]
    offsets = jnp.arange(STRETCH, dtype=jnp.int32)
    positions = (own_stretches[:, None] * STRETCH + offsets[None, :]).reshape(ROWS)
    cosine, sine = angle_tables(positions)
    r = jnp.arange(16, dtype=jnp.int32)
    key_zl = zl ^ (4 * (r & 1)) ^ (2 * ((r >> 1) & 1)) ^ ((r >> 2) & 1)
    key_core = core ^ (r >> 3)
    key_index = y * 16 + key_zl * 2 + key_core
    device = jnp.arange(64, dtype=jnp.int32)
    pick = key_index[:, None, None] == device[None, :, None]
    key_stretch = jnp.sum(jnp.where(pick, stretch_table[None], 0), axis=1).reshape(32)
    query_index = jnp.arange(4, dtype=jnp.int32) * 16 + zl * 2 + core
    pick = query_index[:, None, None] == device[None, :, None]
    query_stretch = jnp.sum(jnp.where(pick, stretch_table[None], 0), axis=1)
    flips = (query_stretch[:, 0] > query_stretch[:, 1]).astype(jnp.int32)
    levels = jnp.stack(
        [jnp.min(query_stretch, axis=1), jnp.max(query_stretch, axis=1)], axis=1
    ).reshape(8)
    ranks = jnp.sum((key_stretch[None, :] < key_stretch[:, None]).astype(jnp.int32), axis=1)
    counts = jnp.sum((key_stretch[None, :] < levels[:, None]).astype(jnp.int32), axis=1)
    plan = jnp.concatenate([ranks, counts, y[None].astype(jnp.int32), flips])
    where = jnp.stack([y, core]).astype(jnp.int32)
    flip = (own_stretches[:1] > own_stretches[1:]).astype(jnp.int32)

    def project(width, across):
        part = pl.pallas_call(
            project_kernel,
            out_shape=jax.ShapeDtypeStruct((4, ROWS, width), f32),
            in_specs=[smem] + [vmem] * 6,
            out_specs=vmem,
            scratch_shapes=[pltpu.VMEM((1024, width), bf16)],
            name="project",
        )(where, *sliced, along_x, across)
        return part

    part = project(2 * HEAD, across)
    query_part = project(HEADS * HEAD, after(across, part))
    part = lax.all_to_all(part, "y", 0, 0)
    key_value = pl.pallas_call(
        key_value_kernel,
        out_shape=jax.ShapeDtypeStruct((ROWS, 2 * HEAD), bf16),
        in_specs=[vmem] * 3,
        out_specs=vmem,
        name="key_value",
    )(part, cosine, sine)
    query_part = lax.all_to_all(after(query_part, key_value), "y", 0, 0)

    step = swap(key_value, "zl", 8, 4)
    step = jnp.concatenate([key_value, step], axis=0)
    near = jnp.concatenate([step, swap(step, "zl", 8, 2)], axis=0)
    far = swap(near, "zl", 8, 1)
    other_near = swap(near, "core", 2, 1)
    other_far = swap(far, "core", 2, 1)

    query = pl.pallas_call(
        query_kernel,
        out_shape=jax.ShapeDtypeStruct((4, HEADS * ROWS, HEAD), bf16),
        in_specs=[smem] + [vmem] * 3,
        out_specs=vmem,
        name="query",
    )(flip, query_part, cosine, sine)
    queries = lax.all_to_all(query, "y", 0, 0)

    keys, values = pl.pallas_call(
        order_kernel,
        out_shape=(
            jax.ShapeDtypeStruct((KEYS, HEAD), bf16),
            jax.ShapeDtypeStruct((KEYS, 2 * HEAD), bf16),
        ),
        in_specs=[smem] + [vmem] * 4,
        out_specs=(vmem, vmem),
        name="order",
    )(plan, near, far, other_near, other_far)
    score_scratch = [pltpu.VMEM((6, HEADS * STRETCH, CHUNK), f32)]
    partial = pl.pallas_call(
        peers_kernel,
        out_shape=jax.ShapeDtypeStruct((4, ROWS, HEADS * HEAD + HEAD), bf16),
        in_specs=[smem] + [vmem] * 3,
        out_specs=vmem,
        scratch_shapes=score_scratch,
        name="peers",
    )(plan, queries, keys, values)
    own_partial = pl.pallas_call(
        own_kernel,
        out_shape=jax.ShapeDtypeStruct((ROWS, HEADS * HEAD + HEAD), bf16),
        in_specs=[smem] + [vmem] * 3,
        out_specs=vmem,
        scratch_shapes=score_scratch,
        name="own",
    )(plan, after(query, partial), keys, values)
    partial = lax.all_to_all(partial, "y", 0, 0)
    attended = pl.pallas_call(
        combine_kernel,
        out_shape=jax.ShapeDtypeStruct((ROWS, HEADS * HEAD), bf16),
        in_specs=[smem] + [vmem] * 2,
        out_specs=vmem,
        name="combine",
    )(plan, partial, own_partial)
    return attended[None]


def solution(mesh):
    fine = Mesh(mesh.devices.reshape(4, 8, 2, 2, 4), ("y", "zl", "core", "zh", "x"))
    ctx = ("y", "zl", "core")
    dp = ("zh", "x")
    placed = (
        P(dp, ctx, None),
        P(),
        P(ctx + dp, None),
        P(ctx + dp, None),
        P(ctx + dp, None),
    )
    return jax.shard_map(
        on_device, mesh=fine, in_specs=placed, out_specs=P(dp, ctx, None), check_vma=False
    )
```

```python
import math

import jax
import jax.numpy as jnp
from jax import lax
from jax.experimental import pallas as pl
from jax.experimental.pallas import tpu as pltpu
from jax.sharding import Mesh, PartitionSpec as P

rope_base = 500000.0
masked_fill = -1e30
HEAD = 128
HEADS = 4
STRETCH = 64
ROWS = 128
KEYS = 2048
CHUNK = 512
score_scale = 1.0 / math.sqrt(HEAD)
exponent_scale = score_scale * math.log2(math.e)

vmem = pl.BlockSpec(memory_space=pltpu.VMEM)
smem = pl.BlockSpec(memory_space=pltpu.SMEM)


def swap(value, axis, size, distance):
    return lax.ppermute(value, axis, [(i, i ^ distance) for i in range(size)])


def spread(value, axis, size):
    copies = jnp.broadcast_to(value[None], (size,) + value.shape)
    return lax.all_to_all(copies, axis, 0, 0)


def angle_tables(positions):
    half = HEAD // 2
    frequency = rope_base ** (-(jnp.arange(half, dtype=jnp.float32) * 2.0 / HEAD))
    angles = positions.astype(jnp.float32)[:, None] * frequency[None, :]
    cosine = jnp.cos(angles)
    sine = jnp.sin(angles)
    return (
        jnp.concatenate([cosine, cosine], axis=1),
        jnp.concatenate([-sine, sine], axis=1),
    )


def gather_rows(weight, source, outer, base, first, width):
    for block in range(outer):
        for group in range(8):
            for half in range(2):
                rows = [
                    source[block * 4 + x, (group * 2 + half) * 8 : (group * 2 + half) * 8 + 8, first : first + width]
                    for x in range(4)
                ]
                target = pl.multiple_of(block * 1024 + group * 128 + half * 32 + base, 32)
                weight[pl.ds(target, 32), :] = jnp.concatenate(rows, axis=0)


def key_value_kernel(where, rows, mine, across, cosine, sine, out, weight):
    core = where[1]
    for far, source in enumerate((mine, across)):
        gather_rows(weight, source, 4, (core ^ far) * 64, 0, 2 * HEAD)
    total = jnp.dot(rows[...], weight[...], preferred_element_type=jnp.float32)
    key = total[:, :HEAD]
    turned = key * cosine[...] + pltpu.roll(key, HEAD // 2, 1) * sine[...]
    out[:, :HEAD] = turned.astype(jnp.bfloat16)
    out[:, HEAD:] = total[:, HEAD:].astype(jnp.bfloat16)


def query_kernel(flip, parts, cosine, sine, out):
    for head in range(HEADS):
        span = slice(head * HEAD, (head + 1) * HEAD)
        total = parts[0, :, span] + parts[1, :, span] + parts[2, :, span] + parts[3, :, span]
        turned = total * cosine[...] + pltpu.roll(total, HEAD // 2, 1) * sine[...]
        turned = turned.astype(jnp.bfloat16)
        for slot in range(2):
            level = slot ^ flip[0]
            row = pl.multiple_of((level * HEADS + head) * STRETCH, STRETCH)
            piece = turned[slot * STRETCH : (slot + 1) * STRETCH]
            for copy in range(4):
                out[copy, pl.ds(row, STRETCH), :] = piece


def project_kernel(where, rows0, rows1, rows2, rows3, mine, across, out, weight):
    y = where[0]
    core = where[1]
    for far, source in enumerate((mine, across)):
        gather_rows(weight, source, 1, (core ^ far) * 64, 0, HEADS * HEAD)
    for shift, rows in enumerate((rows0, rows1, rows2, rows3)):
        out[(y + 4 - shift) % 4] = jnp.dot(
            rows[...], weight[...], preferred_element_type=jnp.float32
        )


def order_kernel(plan, own_near, own_far, other_near, other_far, keys, values):
    pieces = (own_near, own_far, other_near, other_far)
    values[:, HEAD:] = jnp.ones((KEYS, HEAD), jnp.bfloat16)
    for index in range(KEYS // STRETCH):
        piece = pieces[index // 8]
        source = (index % 8) * STRETCH
        target = pl.multiple_of(plan[index] * STRETCH, STRETCH)
        keys[pl.ds(target, STRETCH), :] = piece[source : source + STRETCH, :HEAD]
        values[pl.ds(target, STRETCH), :HEAD] = piece[source : source + STRETCH, HEAD:]


def scores_of(q, keys, low_key):
    return lax.dot_general(
        q, keys[low_key : low_key + CHUNK, :], (((1,), (1,)), ((), ())),
        preferred_element_type=jnp.float32,
    )


def attend_peer(plan, peer, q_low, q_high, keys, values, scores, write):
    rows = HEADS * STRETCH
    here = (plan[40] == peer).astype(jnp.int32)
    in_stretch = lax.broadcasted_iota(jnp.int32, (rows, HEAD), 0) % STRETCH + 1
    lane = lax.broadcasted_iota(jnp.int32, (rows, HEAD), 1)
    slack = in_stretch * here - lane
    small_lane = lax.broadcasted_iota(jnp.int32, (STRETCH, HEAD), 1)
    tops = []
    for level, q in enumerate((q_low, q_high)):
        full = (plan[32 + 2 * peer + level] - 16 * level) * STRETCH
        running = jnp.full((rows, HEAD), -1e20, jnp.float32)
        for block in range(2 * (1 + level)):
            masked = level == 0 or block >= 2
            s = scores_of(q, keys, block * CHUNK)
            for part in range(CHUNK // HEAD):
                lanes = slice(part * HEAD, (part + 1) * HEAD)
                t = s[:, lanes]
                if masked:
                    start = (block % 2) * CHUNK + part * HEAD
                    t = jnp.where(slack > start - full, t, masked_fill)
                scores[2 * level + block, :, lanes] = t
                running = jnp.maximum(running, t)
        tops.append(jnp.max(running, axis=1, keepdims=True))
    for level in range(2):
        top = tops[level]
        acc = jnp.zeros((rows, 2 * HEAD), jnp.float32)
        for block in range(2 * (1 + level)):
            p = jnp.exp2((scores[2 * level + block] - top) * exponent_scale).astype(jnp.bfloat16)
            acc = acc + jnp.dot(
                p, values[block * CHUNK : (block + 1) * CHUNK, :], preferred_element_type=jnp.float32
            )
        total = acc[:, HEAD:]
        mixed = acc[:, :HEAD] / jnp.where(total > 0.0, total, 1.0)
        stats = jnp.zeros((STRETCH, HEAD), jnp.float32)
        row = pl.multiple_of((level ^ plan[41 + peer]) * STRETCH, STRETCH)
        for head in range(HEADS):
            span = slice(head * STRETCH, (head + 1) * STRETCH)
            write(row, slice(head * HEAD, (head + 1) * HEAD), mixed[span].astype(jnp.bfloat16))
            for kind, whole in enumerate((jnp.broadcast_to(top[span], (STRETCH, HEAD)), total[span])):
                rest = whole
                for digit in range(3):
                    part = rest.astype(jnp.bfloat16).astype(jnp.float32)
                    stats = jnp.where(small_lane == head * 6 + kind * 3 + digit, part, stats)
                    rest = rest - part
        write(row, slice(HEADS * HEAD, HEADS * HEAD + HEAD), stats.astype(jnp.bfloat16))


def peers_kernel(plan, query, keys, values, out, scores):
    rows = HEADS * STRETCH
    own = plan[40]
    out[own] = jnp.zeros(out.shape[1:], jnp.bfloat16)

    def body(shift, carried):
        peer = (own + shift) % 4

        def write(row, lanes, value):
            out[peer, pl.ds(row, STRETCH), lanes] = value

        attend_peer(
            plan, peer, query[peer, :rows, :], query[peer, rows:, :], keys, values, scores, write
        )
        return carried

    lax.fori_loop(1, 4, body, 0)


def own_kernel(plan, query, keys, values, out, scores):
    rows = HEADS * STRETCH

    def write(row, lanes, value):
        out[pl.ds(row, STRETCH), lanes] = value

    attend_peer(
        plan, plan[40], query[0, :rows, :], query[0, rows:, :], keys, values, scores, write
    )


def combine_kernel(plan, parts, own, out):
    y = plan[40]
    lane = lax.broadcasted_iota(jnp.int32, (HEAD, 8 * HEAD), 0)
    group = lax.broadcasted_iota(jnp.int32, (HEAD, 8 * HEAD), 1) // HEAD
    pick = (lane // 3 == group).astype(jnp.float32).astype(jnp.bfloat16)
    results = [jnp.where(y == peer, own[...], parts[peer]) for peer in range(4)]
    spread_stats = [
        jnp.dot(result[:, HEADS * HEAD :], pick, preferred_element_type=jnp.float32)
        for result in results
    ]
    for head in range(HEADS):
        tops = [w[:, 2 * head * HEAD : (2 * head + 1) * HEAD] for w in spread_stats]
        totals = [w[:, (2 * head + 1) * HEAD : (2 * head + 2) * HEAD] for w in spread_stats]
        top = jnp.maximum(jnp.maximum(tops[0], tops[1]), jnp.maximum(tops[2], tops[3]))
        weights = [jnp.exp2((tops[k] - top) * exponent_scale) * totals[k] for k in range(4)]
        whole = weights[0] + weights[1] + weights[2] + weights[3]
        mixed = 0.0
        for peer in range(4):
            mixed += weights[peer] * results[peer][:, head * HEAD : (head + 1) * HEAD].astype(jnp.float32)
        out[:, head * HEAD : (head + 1) * HEAD] = (mixed / whole).astype(jnp.bfloat16)


def in_vmem(*values):
    return tuple(pltpu.with_memory_space_constraint(value, pltpu.VMEM) for value in values)


limits = pltpu.CompilerParams(vmem_limit_bytes=16 * 1024 * 1024)


def after(value, *others):
    return lax.optimization_barrier((value,) + others)[0]


def on_device(tokens, stretch_table, query_weight, key_weight, value_weight):
    bf16, f32 = jnp.bfloat16, jnp.float32
    y = lax.axis_index("y")
    zl = lax.axis_index("zl")
    core = lax.axis_index("core")
    rows = tokens[0]
    own = jnp.concatenate([key_weight, value_weight, query_weight], axis=1)
    along_z = spread(own, ("zl", "zh"), 16)
    sliced = []
    for shift in range(4):
        target = (y + shift) % 4
        piece = lax.dynamic_slice_in_dim(rows, target * 1024, 1024, 1)
        if shift:
            piece = lax.ppermute(piece, "y", [(i, (i + shift) % 4) for i in range(4)])
        sliced.append(piece)
    along_z = after(along_z, sliced[1])
    narrow = spread(along_z[:, :, : 2 * HEAD], "x", 4)
    narrow = after(narrow, sliced[3])
    narrow = spread(narrow, "y", 4).reshape(16, ROWS, 2 * HEAD)
    narrow = after(narrow, sliced[2])
    narrow_across = swap(narrow, "core", 2, 1)
    wide, _ = lax.optimization_barrier((along_z[:, :, 2 * HEAD :], narrow))
    wide = spread(wide, "x", 4).reshape(4, ROWS, HEADS * HEAD)

    table = stretch_table.reshape(4, 8, 2, 2)
    own_stretches = table[y, zl, core]
    offsets = jnp.arange(STRETCH, dtype=jnp.int32)
    positions = (own_stretches[:, None] * STRETCH + offsets[None, :]).reshape(ROWS)
    cosine, sine = angle_tables(positions)
    r = jnp.arange(16, dtype=jnp.int32)
    key_zl = zl ^ (4 * (r & 1)) ^ (2 * ((r >> 1) & 1)) ^ ((r >> 2) & 1)
    key_core = core ^ (r >> 3)
    key_index = y * 16 + key_zl * 2 + key_core
    device = jnp.arange(64, dtype=jnp.int32)
    pick = key_index[:, None, None] == device[None, :, None]
    key_stretch = jnp.sum(jnp.where(pick, stretch_table[None], 0), axis=1).reshape(32)
    query_index = jnp.arange(4, dtype=jnp.int32) * 16 + zl * 2 + core
    pick = query_index[:, None, None] == device[None, :, None]
    query_stretch = jnp.sum(jnp.where(pick, stretch_table[None], 0), axis=1)
    flips = (query_stretch[:, 0] > query_stretch[:, 1]).astype(jnp.int32)
    levels = jnp.stack(
        [jnp.min(query_stretch, axis=1), jnp.max(query_stretch, axis=1)], axis=1
    ).reshape(8)
    ranks = jnp.sum((key_stretch[None, :] < key_stretch[:, None]).astype(jnp.int32), axis=1)
    counts = jnp.sum((key_stretch[None, :] < levels[:, None]).astype(jnp.int32), axis=1)
    plan = jnp.concatenate([ranks, counts, y[None].astype(jnp.int32), flips])
    where = jnp.stack([y, core]).astype(jnp.int32)
    flip = (own_stretches[:1] > own_stretches[1:]).astype(jnp.int32)

    key_value = pl.pallas_call(
        key_value_kernel,
        out_shape=pltpu.VMEM((ROWS, 2 * HEAD), bf16),
        in_specs=[smem] + [vmem] * 5,
        out_specs=vmem,
        scratch_shapes=[pltpu.VMEM((4096, 2 * HEAD), bf16)],
        compiler_params=limits,
        name="key_value",
    )(where, *in_vmem(rows, narrow, narrow_across, cosine, sine))
    wide = after(wide, key_value)
    wide_across = swap(wide, "core", 2, 1)
    query_part = pl.pallas_call(
        project_kernel,
        out_shape=pltpu.VMEM((4, ROWS, HEADS * HEAD), f32),
        in_specs=[smem] + [vmem] * 6,
        out_specs=vmem,
        scratch_shapes=[pltpu.VMEM((1024, HEADS * HEAD), bf16)],
        compiler_params=limits,
        name="project",
    )(where, *in_vmem(*sliced, wide, wide_across))
    query_part = lax.all_to_all(query_part, "y", 0, 0)

    step = swap(key_value, "zl", 8, 4)
    step = jnp.concatenate([key_value, step], axis=0)
    near = jnp.concatenate([step, swap(step, "zl", 8, 2)], axis=0)
    far = swap(near, "zl", 8, 1)
    other_near = swap(near, "core", 2, 1)
    other_far = swap(far, "core", 2, 1)

    query = pl.pallas_call(
        query_kernel,
        out_shape=pltpu.VMEM((4, HEADS * ROWS, HEAD), bf16),
        in_specs=[smem] + [vmem] * 3,
        out_specs=vmem,
        compiler_params=limits,
        name="query",
    )(flip, *in_vmem(query_part, cosine, sine))
    queries = lax.all_to_all(query, "y", 0, 0)

    keys, values = pl.pallas_call(
        order_kernel,
        out_shape=(
            pltpu.VMEM((KEYS, HEAD), bf16),
            pltpu.VMEM((KEYS, 2 * HEAD), bf16),
        ),
        in_specs=[smem] + [vmem] * 4,
        out_specs=(vmem, vmem),
        compiler_params=limits,
        name="order",
    )(plan, *in_vmem(near, far, other_near, other_far))
    score_scratch = [pltpu.VMEM((6, HEADS * STRETCH, CHUNK), f32)]
    partial = pl.pallas_call(
        peers_kernel,
        out_shape=pltpu.VMEM((4, ROWS, HEADS * HEAD + HEAD), bf16),
        in_specs=[smem] + [vmem] * 3,
        out_specs=vmem,
        scratch_shapes=score_scratch,
        compiler_params=limits,
        name="peers",
    )(plan, *in_vmem(queries, keys, values))
    own_partial = pl.pallas_call(
        own_kernel,
        out_shape=pltpu.VMEM((ROWS, HEADS * HEAD + HEAD), bf16),
        in_specs=[smem] + [vmem] * 3,
        out_specs=vmem,
        scratch_shapes=score_scratch,
        compiler_params=limits,
        name="own",
    )(plan, *in_vmem(after(query, partial), keys, values))
    partial = lax.all_to_all(partial, "y", 0, 0)
    attended = pl.pallas_call(
        combine_kernel,
        out_shape=jax.ShapeDtypeStruct((ROWS, HEADS * HEAD), bf16),
        in_specs=[smem] + [vmem] * 2,
        out_specs=vmem,
        compiler_params=limits,
        name="combine",
    )(plan, *in_vmem(partial, own_partial))
    return attended[None]


def solution(mesh):
    fine = Mesh(mesh.devices.reshape(4, 8, 2, 2, 4), ("y", "zl", "core", "zh", "x"))
    ctx = ("y", "zl", "core")
    dp = ("zh", "x")
    placed = (
        P(dp, ctx, None),
        P(),
        P(ctx + dp, None),
        P(ctx + dp, None),
        P(ctx + dp, None),
    )
    return jax.shard_map(
        on_device, mesh=fine, in_specs=placed, out_specs=P(dp, ctx, None), check_vma=False
    )
```

```python
import math

import jax
import jax.numpy as jnp
from jax import lax
from jax.experimental import pallas as pl
from jax.experimental.pallas import tpu as pltpu
from jax.sharding import Mesh, PartitionSpec as P

rope_base = 500000.0
masked_fill = -1e30
HEAD = 128
HEADS = 4
STRETCH = 64
ROWS = 128
KEYS = 2048
CHUNK = 512
score_scale = 1.0 / math.sqrt(HEAD)
exponent_scale = score_scale * math.log2(math.e)

vmem = pl.BlockSpec(memory_space=pltpu.VMEM)
smem = pl.BlockSpec(memory_space=pltpu.SMEM)


def swap(value, axis, size, distance):
    return lax.ppermute(value, axis, [(i, i ^ distance) for i in range(size)])


def spread(value, axis, size):
    copies = jnp.broadcast_to(value[None], (size,) + value.shape)
    return lax.all_to_all(copies, axis, 0, 0)


def angle_tables(positions):
    half = HEAD // 2
    frequency = rope_base ** (-(jnp.arange(half, dtype=jnp.float32) * 2.0 / HEAD))
    angles = positions.astype(jnp.float32)[:, None] * frequency[None, :]
    cosine = jnp.cos(angles)
    sine = jnp.sin(angles)
    return (
        jnp.concatenate([cosine, cosine], axis=1),
        jnp.concatenate([-sine, sine], axis=1),
    )


def gather_rows(weight, source, outer, base, first, width):
    for block in range(outer):
        for group in range(8):
            for half in range(2):
                rows = [
                    source[block * 4 + x, (group * 2 + half) * 8 : (group * 2 + half) * 8 + 8, first : first + width]
                    for x in range(4)
                ]
                target = pl.multiple_of(block * 1024 + group * 128 + half * 32 + base, 32)
                weight[pl.ds(target, 32), :] = jnp.concatenate(rows, axis=0)


def key_value_kernel(where, rows, mine, across, cosine, sine, out, weight):
    core = where[1]
    for far, source in enumerate((mine, across)):
        gather_rows(weight, source, 4, (core ^ far) * 64, 0, 2 * HEAD)
    total = jnp.dot(rows[...], weight[...], preferred_element_type=jnp.float32)
    key = total[:, :HEAD]
    turned = key * cosine[...] + pltpu.roll(key, HEAD // 2, 1) * sine[...]
    out[:, :HEAD] = turned.astype(jnp.bfloat16)
    out[:, HEAD:] = total[:, HEAD:].astype(jnp.bfloat16)


def query_kernel(flip, parts, cosine, sine, out):
    for head in range(HEADS):
        span = slice(head * HEAD, (head + 1) * HEAD)
        total = parts[0, :, span] + parts[1, :, span] + parts[2, :, span] + parts[3, :, span]
        turned = total * cosine[...] + pltpu.roll(total, HEAD // 2, 1) * sine[...]
        turned = turned.astype(jnp.bfloat16)
        for slot in range(2):
            level = slot ^ flip[0]
            row = pl.multiple_of((level * HEADS + head) * STRETCH, STRETCH)
            piece = turned[slot * STRETCH : (slot + 1) * STRETCH]
            for copy in range(4):
                out[copy, pl.ds(row, STRETCH), :] = piece


def project_kernel(where, rows0, rows1, rows2, rows3, mine, across, out, weight):
    y = where[0]
    core = where[1]
    for far, source in enumerate((mine, across)):
        gather_rows(weight, source, 1, (core ^ far) * 64, 0, HEADS * HEAD)
    for shift, rows in enumerate((rows0, rows1, rows2, rows3)):
        out[(y + 4 - shift) % 4] = jnp.dot(
            rows[...], weight[...], preferred_element_type=jnp.float32
        )


def order_kernel(plan, own_near, own_far, other_near, other_far, keys, values):
    pieces = (own_near, own_far, other_near, other_far)
    values[:, HEAD:] = jnp.ones((KEYS, HEAD), jnp.bfloat16)
    for index in range(KEYS // STRETCH):
        piece = pieces[index // 8]
        source = (index % 8) * STRETCH
        target = pl.multiple_of(plan[index] * STRETCH, STRETCH)
        keys[pl.ds(target, STRETCH), :] = piece[source : source + STRETCH, :HEAD]
        values[pl.ds(target, STRETCH), :HEAD] = piece[source : source + STRETCH, HEAD:]


def scores_of(q, keys, low_key):
    return lax.dot_general(
        q, keys[low_key : low_key + CHUNK, :], (((1,), (1,)), ((), ())),
        preferred_element_type=jnp.float32,
    )


def attend_peer(plan, peer, q_low, q_high, keys, values, scores, write):
    rows = HEADS * STRETCH
    here = (plan[40] == peer).astype(jnp.int32)
    in_stretch = lax.broadcasted_iota(jnp.int32, (rows, HEAD), 0) % STRETCH + 1
    lane = lax.broadcasted_iota(jnp.int32, (rows, HEAD), 1)
    slack = in_stretch * here - lane
    small_lane = lax.broadcasted_iota(jnp.int32, (STRETCH, HEAD), 1)
    tops = []
    for level, q in enumerate((q_low, q_high)):
        full = (plan[32 + 2 * peer + level] - 16 * level) * STRETCH
        running = jnp.full((rows, HEAD), -1e20, jnp.float32)
        for block in range(2 * (1 + level)):
            masked = level == 0 or block >= 2
            s = scores_of(q, keys, block * CHUNK)
            for part in range(CHUNK // HEAD):
                lanes = slice(part * HEAD, (part + 1) * HEAD)
                t = s[:, lanes]
                if masked:
                    start = (block % 2) * CHUNK + part * HEAD
                    t = jnp.where(slack > start - full, t, masked_fill)
                scores[2 * level + block, :, lanes] = t
                running = jnp.maximum(running, t)
        tops.append(jnp.max(running, axis=1, keepdims=True))
    for level in range(2):
        top = tops[level]
        acc = jnp.zeros((rows, 2 * HEAD), jnp.float32)
        for block in range(2 * (1 + level)):
            p = jnp.exp2((scores[2 * level + block] - top) * exponent_scale).astype(jnp.bfloat16)
            acc = acc + jnp.dot(
                p, values[block * CHUNK : (block + 1) * CHUNK, :], preferred_element_type=jnp.float32
            )
        total = acc[:, HEAD:]
        mixed = acc[:, :HEAD] / jnp.where(total > 0.0, total, 1.0)
        stats = jnp.zeros((STRETCH, HEAD), jnp.float32)
        row = pl.multiple_of((level ^ plan[41 + peer]) * STRETCH, STRETCH)
        for head in range(HEADS):
            span = slice(head * STRETCH, (head + 1) * STRETCH)
            write(row, slice(head * HEAD, (head + 1) * HEAD), mixed[span].astype(jnp.bfloat16))
            for kind, whole in enumerate((jnp.broadcast_to(top[span], (STRETCH, HEAD)), total[span])):
                rest = whole
                for digit in range(3):
                    part = rest.astype(jnp.bfloat16).astype(jnp.float32)
                    stats = jnp.where(small_lane == head * 6 + kind * 3 + digit, part, stats)
                    rest = rest - part
        write(row, slice(HEADS * HEAD, HEADS * HEAD + HEAD), stats.astype(jnp.bfloat16))


def peers_kernel(plan, query, keys, values, out, scores):
    rows = HEADS * STRETCH
    own = plan[40]
    out[own] = jnp.zeros(out.shape[1:], jnp.bfloat16)

    def body(shift, carried):
        peer = (own + shift) % 4

        def write(row, lanes, value):
            out[peer, pl.ds(row, STRETCH), lanes] = value

        attend_peer(
            plan, peer, query[peer, :rows, :], query[peer, rows:, :], keys, values, scores, write
        )
        return carried

    lax.fori_loop(1, 4, body, 0)


def own_kernel(plan, query, keys, values, out, scores):
    rows = HEADS * STRETCH

    def write(row, lanes, value):
        out[pl.ds(row, STRETCH), lanes] = value

    attend_peer(
        plan, plan[40], query[0, :rows, :], query[0, rows:, :], keys, values, scores, write
    )


def combine_kernel(plan, parts, own, out):
    y = plan[40]
    lane = lax.broadcasted_iota(jnp.int32, (HEAD, 8 * HEAD), 0)
    group = lax.broadcasted_iota(jnp.int32, (HEAD, 8 * HEAD), 1) // HEAD
    pick = (lane // 3 == group).astype(jnp.float32).astype(jnp.bfloat16)
    results = [jnp.where(y == peer, own[...], parts[peer]) for peer in range(4)]
    spread_stats = [
        jnp.dot(result[:, HEADS * HEAD :], pick, preferred_element_type=jnp.float32)
        for result in results
    ]
    for head in range(HEADS):
        tops = [w[:, 2 * head * HEAD : (2 * head + 1) * HEAD] for w in spread_stats]
        totals = [w[:, (2 * head + 1) * HEAD : (2 * head + 2) * HEAD] for w in spread_stats]
        top = jnp.maximum(jnp.maximum(tops[0], tops[1]), jnp.maximum(tops[2], tops[3]))
        weights = [jnp.exp2((tops[k] - top) * exponent_scale) * totals[k] for k in range(4)]
        whole = weights[0] + weights[1] + weights[2] + weights[3]
        mixed = 0.0
        for peer in range(4):
            mixed += weights[peer] * results[peer][:, head * HEAD : (head + 1) * HEAD].astype(jnp.float32)
        out[:, head * HEAD : (head + 1) * HEAD] = (mixed / whole).astype(jnp.bfloat16)


def in_vmem(*values):
    return tuple(pltpu.with_memory_space_constraint(value, pltpu.VMEM) for value in values)


limits = pltpu.CompilerParams(vmem_limit_bytes=16 * 1024 * 1024)


def after(value, *others):
    return lax.optimization_barrier((value,) + others)[0]


def on_device(tokens, stretch_table, query_weight, key_weight, value_weight):
    bf16, f32 = jnp.bfloat16, jnp.float32
    y = lax.axis_index("y")
    zl = lax.axis_index("zl")
    core = lax.axis_index("core")
    rows = tokens[0]
    own = jnp.concatenate([key_weight, value_weight, query_weight], axis=1)
    along_z = spread(own, ("zl", "zh"), 16)
    sliced = []
    for shift in range(4):
        target = (y + shift) % 4
        piece = lax.dynamic_slice_in_dim(rows, target * 1024, 1024, 1)
        if shift:
            piece = lax.ppermute(piece, "y", [(i, (i + shift) % 4) for i in range(4)])
        sliced.append(piece)
    along_z = after(along_z, sliced[1], sliced[2])
    along_x = after(spread(along_z, "x", 4), sliced[3]).reshape(4, ROWS, 768)
    wide = along_x[:, :, 2 * HEAD :]
    wide_across = swap(wide, "core", 2, 1)
    narrow = spread(along_x[:, :, : 2 * HEAD], "y", 4).reshape(16, ROWS, 2 * HEAD)

    table = stretch_table.reshape(4, 8, 2, 2)
    own_stretches = table[y, zl, core]
    offsets = jnp.arange(STRETCH, dtype=jnp.int32)
    positions = (own_stretches[:, None] * STRETCH + offsets[None, :]).reshape(ROWS)
    cosine, sine = angle_tables(positions)
    r = jnp.arange(16, dtype=jnp.int32)
    key_zl = zl ^ (4 * (r & 1)) ^ (2 * ((r >> 1) & 1)) ^ ((r >> 2) & 1)
    key_core = core ^ (r >> 3)
    key_index = y * 16 + key_zl * 2 + key_core
    device = jnp.arange(64, dtype=jnp.int32)
    pick = key_index[:, None, None] == device[None, :, None]
    key_stretch = jnp.sum(jnp.where(pick, stretch_table[None], 0), axis=1).reshape(32)
    query_index = jnp.arange(4, dtype=jnp.int32) * 16 + zl * 2 + core
    pick = query_index[:, None, None] == device[None, :, None]
    query_stretch = jnp.sum(jnp.where(pick, stretch_table[None], 0), axis=1)
    flips = (query_stretch[:, 0] > query_stretch[:, 1]).astype(jnp.int32)
    levels = jnp.stack(
        [jnp.min(query_stretch, axis=1), jnp.max(query_stretch, axis=1)], axis=1
    ).reshape(8)
    ranks = jnp.sum((key_stretch[None, :] < key_stretch[:, None]).astype(jnp.int32), axis=1)
    counts = jnp.sum((key_stretch[None, :] < levels[:, None]).astype(jnp.int32), axis=1)
    plan = jnp.concatenate([ranks, counts, y[None].astype(jnp.int32), flips])
    where = jnp.stack([y, core]).astype(jnp.int32)
    flip = (own_stretches[:1] > own_stretches[1:]).astype(jnp.int32)

    query_part = pl.pallas_call(
        project_kernel,
        out_shape=pltpu.VMEM((4, ROWS, HEADS * HEAD), f32),
        in_specs=[smem] + [vmem] * 6,
        out_specs=vmem,
        scratch_shapes=[pltpu.VMEM((1024, HEADS * HEAD), bf16)],
        compiler_params=limits,
        name="project",
    )(where, *in_vmem(*sliced, wide, wide_across))
    narrow, query_part = lax.optimization_barrier((narrow, query_part))
    narrow_across = swap(narrow, "core", 2, 1)
    query_part = lax.all_to_all(query_part, "y", 0, 0)
    key_value = pl.pallas_call(
        key_value_kernel,
        out_shape=pltpu.VMEM((ROWS, 2 * HEAD), bf16),
        in_specs=[smem] + [vmem] * 5,
        out_specs=vmem,
        scratch_shapes=[pltpu.VMEM((4096, 2 * HEAD), bf16)],
        compiler_params=limits,
        name="key_value",
    )(where, *in_vmem(rows, narrow, narrow_across, cosine, sine))

    step = swap(key_value, "zl", 8, 4)
    step = jnp.concatenate([key_value, step], axis=0)
    near = jnp.concatenate([step, swap(step, "zl", 8, 2)], axis=0)
    far = swap(near, "zl", 8, 1)
    other_near = swap(near, "core", 2, 1)
    other_far = swap(far, "core", 2, 1)

    query = pl.pallas_call(
        query_kernel,
        out_shape=pltpu.VMEM((4, HEADS * ROWS, HEAD), bf16),
        in_specs=[smem] + [vmem] * 3,
        out_specs=vmem,
        compiler_params=limits,
        name="query",
    )(flip, *in_vmem(after(query_part, key_value), cosine, sine))
    queries = lax.all_to_all(query, "y", 0, 0)

    keys, values = pl.pallas_call(
        order_kernel,
        out_shape=(
            pltpu.VMEM((KEYS, HEAD), bf16),
            pltpu.VMEM((KEYS, 2 * HEAD), bf16),
        ),
        in_specs=[smem] + [vmem] * 4,
        out_specs=(vmem, vmem),
        compiler_params=limits,
        name="order",
    )(plan, *in_vmem(near, far, other_near, other_far))
    score_scratch = [pltpu.VMEM((6, HEADS * STRETCH, CHUNK), f32)]
    partial = pl.pallas_call(
        peers_kernel,
        out_shape=pltpu.VMEM((4, ROWS, HEADS * HEAD + HEAD), bf16),
        in_specs=[smem] + [vmem] * 3,
        out_specs=vmem,
        scratch_shapes=score_scratch,
        compiler_params=limits,
        name="peers",
    )(plan, *in_vmem(queries, keys, values))
    own_partial = pl.pallas_call(
        own_kernel,
        out_shape=pltpu.VMEM((ROWS, HEADS * HEAD + HEAD), bf16),
        in_specs=[smem] + [vmem] * 3,
        out_specs=vmem,
        scratch_shapes=score_scratch,
        compiler_params=limits,
        name="own",
    )(plan, *in_vmem(after(query, partial), keys, values))
    partial = lax.all_to_all(partial, "y", 0, 0)
    attended = pl.pallas_call(
        combine_kernel,
        out_shape=jax.ShapeDtypeStruct((ROWS, HEADS * HEAD), bf16),
        in_specs=[smem] + [vmem] * 2,
        out_specs=vmem,
        compiler_params=limits,
        name="combine",
    )(plan, *in_vmem(partial, own_partial))
    return attended[None]


def solution(mesh):
    fine = Mesh(mesh.devices.reshape(4, 8, 2, 2, 4), ("y", "zl", "core", "zh", "x"))
    ctx = ("y", "zl", "core")
    dp = ("zh", "x")
    placed = (
        P(dp, ctx, None),
        P(),
        P(ctx + dp, None),
        P(ctx + dp, None),
        P(ctx + dp, None),
    )
    return jax.shard_map(
        on_device, mesh=fine, in_specs=placed, out_specs=P(dp, ctx, None), check_vma=False
    )
```
